512 devices in a mesh: tensor: 64 (over x, z_lo, core), expert: 8 (over z_hi, y).
Axes of the slice: x: 4, y: 4, z: 16 (z_hi: 2, z_lo: 8; z = z_hi * 8 + z_lo), core: 2. Of those that a mesh axis runs over, the one named last changes fastest.
Arguments:
- acts: bfloat16 [384, 3072], P('expert', 'tensor'), may hold values from -6 to 6
- grad_out: bfloat16 [384, 3072], P('expert', 'tensor'), may hold values from -6 to 6
- routing: int32 [384, 2], P('expert'), may hold values from 0 to 7, all different within a row; in each aligned block of 48 rows (0 to 47, 48 to 95, ...) at most 24 rows name the same one
- gates: float32 [384, 2], P('expert'), may hold values from 0.1 to 1
- w_gate: bfloat16 [8, 3072, 8192], P('expert', None, 'tensor'), may hold values from -0.109375 to 0.109375
- w_up: bfloat16 [8, 3072, 8192], P('expert', None, 'tensor'), may hold values from -0.109375 to 0.109375
- w_down: bfloat16 [8, 8192, 3072], P('expert', 'tensor'), may hold values from -0.0625 to 0.0625
Outputs:
- grad_gate: bfloat16 [8, 3072, 8192], P('expert', None, 'tensor')
- grad_up: bfloat16 [8, 3072, 8192], P('expert', None, 'tensor')
- grad_down: bfloat16 [8, 8192, 3072], P('expert', 'tensor')
- grad_acts: bfloat16 [384, 3072], P('expert', 'tensor')
The draws below stay inside these ranges and needn't reach their ends.
Inputs may be any that keep to these rules, and one draw needn't show every extreme that they name: `routing`: within the tokens of one owner group (aligned blocks of 48 rows) no expert is named more than 24 times, a bound that some block reaches; a token's two experts differ.
All inputs are finite; a program needn't handle non-finite values.
Results may differ from the reference program's by a relative error of at most 0.02.
Values may be sent and summed in bfloat16 or wider, within the bound.
A program may use at most 64 MiB of HBM per device.

```python
import math
import jax
import jax.numpy as jnp
import numpy as np
from jax import lax

D = 3072
FF = 8192
TOK_DEV = 48
EXPERTS = 8
CAP = 24
SLOTS = 192
TOKENS = 384
N_EXPERT = 8


def level_of(key, shape, pieces, low, largest):
    def one(dim, shards_of):
        draws = jax.random.uniform(jax.random.fold_in(jax.random.fold_in(key, 6), dim), (shards_of,), jnp.float32, low / len(pieces), largest / len(pieces))
        return jnp.repeat(jnp.exp(draws), shape[dim] // shards_of).reshape((-1,) + (1,) * (len(shape) - dim - 1))

    loudness = one(*pieces[0])
    for cut in pieces[1:]:
        loudness = loudness * one(*cut)
    return loudness


def deal_out(own_key, own, number, rows, number_of, top, most, slope):
    ranking = jax.random.permutation(own_key, number_of)
    crowded, usual = portions_of(number_of, rows * top, most, slope, True), portions_of(number_of, rows * top, most, slope, False)
    places = jnp.arange(number_of)

    def named(sizes, turn):
        used = int((sizes > 0).sum())
        fixed = max(1, used // 4)
        passed = fixed + (places - fixed + turn * (used - fixed)) % max(1, number_of - fixed)
        return jnp.zeros((number_of,), jnp.int32).at[ranking[jnp.where(places < fixed, places, passed)]].set(jnp.asarray(sizes, jnp.int32))

    sizes = jnp.where(number % 4 == 0, named(crowded, number // 4), named(usual, number - number // 4 - 1))
    mixed = jax.random.permutation(jax.random.fold_in(own, 3), number_of)
    source_of, sink = mixed[0:number_of // 2 * 2:2], mixed[1:number_of // 2 * 2:2]
    room = jnp.minimum(sizes[source_of] - 1, most - sizes[sink]) // 2
    room = jnp.where((source_of == ranking[0]) | (sink == ranking[0]) | (sizes[sink] == 0), 0, jnp.maximum(room, 0))
    passed = jax.random.randint(jax.random.fold_in(own, 4), (number_of // 2,), 0, 1 << 20) % (room + 1)
    sizes = sizes.at[source_of].add(-passed).at[sink].add(passed)
    labels = jnp.searchsorted(jnp.cumsum(sizes), jnp.arange(rows * top), side="right").astype(jnp.int32)
    grid = labels.reshape(top, rows).T
    grid = grid[jax.random.permutation(jax.random.fold_in(own, 1), rows)]
    turn = jax.random.randint(jax.random.fold_in(own, 2), (rows, 1), 0, top)
    return jnp.take_along_axis(grid, (jnp.arange(top)[None, :] + turn) % top, axis=1)


def portions_of(amount, total, reach, skew, full):
    weights = [(1 << 20) // math.isqrt(grade ** skew) + 1 for grade in range(1, amount + 1)]
    largest = reach if full else min(reach, max(-(-total // amount), total * weights[0] // sum(weights)))
    least = 1 if total - largest >= amount - 1 else 0
    given, spare = [largest] + [least] * (amount - 1), total - largest - least * (amount - 1)
    while spare > 0:
        movable = [i for i in range(1, amount) if given[i] < largest] or [i for i in range(1, amount) if given[i] < reach]
        pool, remaining = sum([weights[i] for i in movable]), spare
        for i in movable:
            extra = min(reach - given[i], max(1, remaining * weights[i] // pool), spare)
            given[i] = given[i] + extra
            spare = spare - extra
    return np.array(given)


def normal_values(own_key, shape, deviation, limit, shards=(), kind=jnp.bfloat16):
    array = jax.random.normal(own_key, shape, jnp.float32) * deviation
    if len(shards) > 0:
        array = level_of(own_key, shape, shards, -0.22, 0.18) * array
    return jnp.clip(array, min=-limit, max=limit).astype(kind)


def setup_inputs(seed: int = 0) -> dict:
    arg_keys = jax.random.split(jax.random.key(seed), 8)
    acts = normal_values(arg_keys[0], (TOKENS, D), 1.0, 6.0, ((0, 8), (1, 64)))
    grad_out = normal_values(arg_keys[1], (TOKENS, D), 1.0, 6.0, ((0, 8), (1, 64)))
    routing_keys = jax.random.split(jax.random.fold_in(arg_keys[2], 1), TOKENS // TOK_DEV)
    routing_turns = jax.random.permutation(jax.random.fold_in(arg_keys[2], 3), TOKENS // TOK_DEV)
    routing = jax.vmap(lambda own, number: deal_out(jax.random.fold_in(arg_keys[2], 2), own, number, TOK_DEV, EXPERTS, 2, CAP, 2))(routing_keys, routing_turns).reshape((TOKENS, 2))
    gates = jnp.clip(0.1 + 0.9 * jax.random.uniform(arg_keys[3], (TOKENS, 2), jnp.float32) ** level_of(arg_keys[3], (TOKENS, 2), ((0, 8),), -0.2, 0.2), 0.1, 1.0)
    w_gate = normal_values(arg_keys[4], (EXPERTS, D, FF), D ** -0.5, 0.109375, ((0, 8), (2, 64)))
    w_up = normal_values(arg_keys[5], (EXPERTS, D, FF), D ** -0.5, 0.109375, ((0, 8), (2, 64)))
    w_down = normal_values(arg_keys[6], (EXPERTS, FF, D), FF ** -0.5, 0.0625, ((0, 8), (1, 64)))
    return {"acts": acts, "grad_out": grad_out, "routing": routing, "gates": gates, "w_gate": w_gate, "w_up": w_up, "w_down": w_down}


def dispatch_table(routing, gates, experts, capacity):
    tok_count = routing.shape[0]
    entries = routing.reshape(-1)
    chosen = (entries[:, None] == jnp.arange(experts, dtype=jnp.int32)[None, :]).astype(jnp.int32)
    earlier = jnp.cumsum(chosen, axis=0) - chosen
    position = jnp.sum(earlier * chosen, axis=1)
    in_slot = (position[:, None] == jnp.arange(capacity, dtype=jnp.int32)[None, :]).astype(jnp.float32)
    placed = chosen.astype(jnp.float32)[:, :, None] * in_slot[:, None, :]
    placed = placed.reshape(tok_count, 2, experts, capacity)
    table = jnp.sum(placed, axis=1)
    gate_slot = jnp.einsum("tkec,tk->ec", placed, gates.astype(jnp.float32))
    return table, gate_slot


def expert_backward(operands):
    rows_acts, rows_grad, gate_weight, up_weight, down_weight = operands
    gate_pre = jnp.dot(rows_acts, gate_weight, preferred_element_type=jnp.float32)
    up_pre = jnp.dot(rows_acts, up_weight, preferred_element_type=jnp.float32)
    gate_sig = jax.nn.sigmoid(gate_pre)
    gate_act = gate_pre * gate_sig
    hidden = (gate_act * up_pre).astype(jnp.bfloat16)
    grad_hidden = jnp.dot(rows_grad, down_weight.T, preferred_element_type=jnp.float32)
    grad_up_pre = (grad_hidden * gate_act).astype(jnp.bfloat16)
    grad_gate_pre = (grad_hidden * up_pre * gate_sig * (1.0 + gate_pre * (1.0 - gate_sig))).astype(jnp.bfloat16)
    grad_down = jnp.dot(hidden.T, rows_grad, preferred_element_type=jnp.float32).astype(jnp.bfloat16)
    grad_gate = jnp.dot(rows_acts.T, grad_gate_pre, preferred_element_type=jnp.float32).astype(jnp.bfloat16)
    grad_up = jnp.dot(rows_acts.T, grad_up_pre, preferred_element_type=jnp.float32).astype(jnp.bfloat16)
    slot_input = jnp.dot(grad_gate_pre, gate_weight.T, preferred_element_type=jnp.float32)
    slot_input = slot_input + jnp.dot(grad_up_pre, up_weight.T, preferred_element_type=jnp.float32)
    return grad_gate, grad_up, grad_down, slot_input.astype(jnp.bfloat16)


def group_table(group_routing, group_gates):
    return dispatch_table(group_routing, group_gates, EXPERTS, CAP)


def reference(acts, grad_out, routing, gates, w_gate, w_up, w_down):
    acts_group = acts.reshape(N_EXPERT, TOK_DEV, D).astype(jnp.float32)
    grad_group = grad_out.reshape(N_EXPERT, TOK_DEV, D).astype(jnp.float32)
    table, gate_slot = jax.vmap(group_table)(routing.reshape(N_EXPERT, TOK_DEV, 2), gates.reshape(N_EXPERT, TOK_DEV, 2))
    slot_acts = jnp.einsum("gtec,gtd->egcd", table, acts_group).astype(jnp.bfloat16)
    slot_grad = jnp.einsum("gtec,gtd->egcd", table, grad_group)
    slot_grad = (slot_grad * jnp.transpose(gate_slot, (1, 0, 2))[:, :, :, None]).astype(jnp.bfloat16)
    rows_acts = slot_acts.reshape(EXPERTS, SLOTS, D)
    rows_grad = slot_grad.reshape(EXPERTS, SLOTS, D)
    grad_gate, grad_up, grad_down, slot_input = lax.map(expert_backward, (rows_acts, rows_grad, w_gate, w_up, w_down))
    slot_input = slot_input.reshape(EXPERTS, N_EXPERT, CAP, D).astype(jnp.float32)
    grad_acts = jnp.einsum("gtec,egcd->gtd", table, slot_input).astype(jnp.bfloat16).reshape(TOKENS, D)
    return grad_gate, grad_up, grad_down, grad_acts
```

```python
import jax
import jax.numpy as jnp
from jax import lax
from jax.experimental import pallas as pl
from jax.experimental.pallas import tpu as pltpu
from jax.sharding import PartitionSpec as P

NX, NZ, NC = 4, 8, 2
NH, NY = 2, 4
F = 48
T = 48
CAP = 24
E = NH * NY
ROWS = E * 2 * CAP
H = 128
K = NZ * NC * F
BF = jnp.bfloat16
F32 = jnp.float32
MESH = pl.DeviceIdType.MESH


def iota(shape, dim):
    return lax.broadcasted_iota(jnp.int32, shape, dim)


def split_rows(i):
    group = (i * 1366) >> 16
    rest = i - group * (2 * CAP)
    half = (rest >= CAP).astype(jnp.int32)
    return group, half, rest - half * CAP


def mm(a, b):
    return jnp.dot(a, b, preferred_element_type=F32)


def nt(a, b):
    return lax.dot_general(a, b, (((1,), (1,)), ((), ())), preferred_element_type=F32)


def kernel(
    acts, grad, routing, gates, wg, wu, wd,
    o_gate, o_up, o_down, o_acts,
    wgu, w3, send, recv, ag, acc, a01, hs, part, sib, xs, xr, zs, zr, back_s, back_r,
    s_w, s_a2a, r_a2a, r_ag, s_agz, s_agx, s_agc,
    s_sib, r_sib, s_x, r_x, s_z, r_z, s_back, r_back,
):
    tensor, expert = lax.axis_index("tensor"), lax.axis_index("expert")
    x, z, c = tensor // (NZ * NC), (tensor // NC) % NZ, tensor % NC
    zh, y = expert // NY, expert % NY

    def dev(x_, z_, c_, zh_, y_):
        return ((x_ * NZ + z_) * NC + c_, zh_ * NY + y_)

    def remote(src, dst, ss, rs, to):
        return pltpu.make_async_remote_copy(
            src_ref=src, dst_ref=dst, send_sem=ss, recv_sem=rs, device_id=to, device_id_type=MESH
        )

    sibling = dev(x, z, 1 - c, zh, y)

    barrier = pltpu.get_barrier_semaphore()

    def greet(to):
        pl.semaphore_signal(barrier, inc=1, device_id=to, device_id_type=MESH)

    for h in range(NH):
        for k in range(NY):
            if h or k:
                for cc in range(NC):
                    greet(dev(x, z, cc, (zh + h) % NH, (y + k) % NY))
    for k in range(1, NZ):
        greet(dev(x, (z + k) % NZ, c, zh, y))
    for k in range(1, NX):
        greet(dev((x + k) % NX, z, c, zh, y))
    greet(sibling)

    w_copies = [
        pltpu.make_async_copy(wg, wgu.at[:, :, :, :, pl.ds(0, H)], s_w.at[0]),
        pltpu.make_async_copy(wu, wgu.at[:, :, :, :, pl.ds(H, H)], s_w.at[1]),
    ] + [
        pltpu.make_async_copy(wd.at[:, pl.ds(q * K, K)], w3.at[q, pl.ds(2 * H, H), :], s_w.at[2 + q])
        for q in range(NX)
    ]
    for cp in w_copies:
        cp.start()

    r = routing[...]
    g = gates[...]
    r0, r1 = r[:, 0:1], r[:, 1:2]
    names = iota((T, E), 1)
    c0, c1 = (r0 == names).astype(F32), (r1 == names).astype(F32)
    before = (iota((T, T), 1) < iota((T, T), 0)).astype(BF)
    earlier = mm(before, (c0 + c1).astype(BF))
    pos0 = jnp.sum(earlier * c0, axis=1, keepdims=True)
    pos1 = jnp.sum((earlier + c0) * c1, axis=1, keepdims=True)
    key0 = jnp.where(pos0 < CAP, r0.astype(F32) * CAP + pos0, -1.0)
    key1 = jnp.where(pos1 < CAP, r1.astype(F32) * CAP + pos1, -1.0)
    eye = (iota((T, T), 0) == iota((T, T), 1)).astype(F32)

    def as_row(col):
        return jnp.sum(eye * col, axis=0, keepdims=True)

    group_c, half_c, slot_c = split_rows(iota((ROWS, 1), 0))
    want = (group_c * CAP + slot_c).astype(F32)
    m0 = (want == as_row(key0)).astype(F32)
    m1 = (want == as_row(key1)).astype(F32)
    gate_slot = jnp.sum(m0 * as_row(g[:, 0:1]) + m1 * as_row(g[:, 1:2]), axis=1, keepdims=True)
    onehot = (m0 + m1).astype(BF)
    rows = jnp.where(half_c == 0, mm(onehot, acts[...]), mm(onehot, grad[...]) * gate_slot)
    rows = jnp.concatenate([rows, jnp.zeros((ROWS, 128 - F), F32)], axis=1)
    send[...] = rows.astype(BF).reshape(E, 2 * CAP, 128)

    group_r, half_r, slot_r = split_rows(iota((1, ROWS), 1))
    want_r = (group_r * CAP + slot_r).astype(F32)
    mine = jnp.logical_and(jnp.logical_or(want_r == key0, want_r == key1), half_r == c)
    combine = mine.astype(BF)

    pl.semaphore_wait(barrier, 2 * (E - 1) + (NZ - 1) + (NX - 1) + 1)

    a2a = []
    for h in reversed(range(NH)):
        for k in range(NY):
            to_h, to_y = (zh + h) % NH, (y + k) % NY
            src, dst = send.at[to_h * NY + to_y], recv.at[h * NY + y]
            i = h * NY + k
            if h or k:
                from_y = (y + NY - k) % NY
                cp = remote(src, dst, s_a2a.at[i], r_a2a.at[i], dev(x, z, c, to_h, to_y))
            else:
                cp = pltpu.make_async_copy(src, dst, s_a2a.at[i])
            cp.start()
            a2a.append(cp)

    for cp in w_copies:
        cp.wait()
    for q in range(NX):
        w3[q, pl.ds(0, 2 * H), :] = wgu[q].reshape(K, 2 * H).T
    for cp in a2a:
        cp.wait()

    pick = (iota((F, 128), 0) == iota((F, 128), 1)).astype(BF)
    ag[x, z, c] = nt(pick, recv[...].reshape(ROWS, 128)).astype(BF)

    def ag_copy(bx, bz, ss, to):
        blk = ag.at[bx, bz, c]
        return remote(blk, blk, ss, r_ag.at[(bx * NZ + bz) * NC + c], to)

    def ag_arrived(bx, bz, bc):
        blk = ag.at[bx, bz, bc]
        remote(blk, blk, s_agz.at[0], r_ag.at[(bx * NZ + bz) * NC + bc], sibling).wait_recv()

    def z_send(k, _):
        ag_copy(x, z, s_agz.at[k], dev(x, (z + k) % NZ, c, zh, y)).start()
        return 0

    lax.fori_loop(1, NZ, z_send, 0)

    def x_send(bz):
        for k in (2, 1, 3):
            ag_copy(x, bz, s_agx.at[k * NZ + bz], dev((x + k) % NX, z, c, zh, y)).start()
        ag_copy(x, bz, s_agc.at[x * NZ + bz], sibling).start()

    x_send(z)

    def z_recv(k, _):
        bz = (z + k) % NZ
        ag_arrived(x, bz, c)
        x_send(bz)
        return 0

    lax.fori_loop(1, NZ, z_recv, 0)

    def block_dot(bx):
        return mm(w3[bx], ag[bx].reshape(K, ROWS))

    for k in (0, 1, 3, 2):
        bx = (x + k) % NX
        if k:
            def pass_on(i, _):
                ag_arrived(bx, (z + i) % NZ, c)
                ag_copy(bx, (z + i) % NZ, s_agc.at[bx * NZ + (z + i) % NZ], sibling).start()
                return 0

            lax.fori_loop(0, NZ, pass_on, 0)

        def other_core(i, _):
            ag_arrived(bx, i, 1 - c)
            return 0

        lax.fori_loop(0, NZ, other_core, 0)
        if k:
            acc[...] += block_dot(bx)
        else:
            acc[...] = block_dot(bx)

    _, lane_half, _ = split_rows(iota((H, ROWS), 1))
    is_x = lane_half == 0
    gate_pre, up_pre = acc[pl.ds(0, H), :], acc[pl.ds(H, H), :]
    grad_hidden = pltpu.roll(acc[pl.ds(2 * H, H), :], ROWS - CAP, 1)
    sig = 1.0 / (1.0 + jnp.exp(-gate_pre))
    act = gate_pre * sig
    zero = jnp.zeros((H, ROWS), F32)
    hidden = jnp.where(is_x, act * up_pre, zero)
    gup = jnp.where(is_x, grad_hidden * act, zero)
    ggp = jnp.where(is_x, grad_hidden * up_pre * sig * (1.0 + gate_pre * (1.0 - sig)), zero)
    gg = jnp.concatenate([ggp, gup], axis=0)
    a01[0] = gg.astype(BF)
    a01[1] = pltpu.roll(gg, CAP, 1).astype(BF)

    sib_copies, x_copies = {}, {}
    for k in (2, 1, 3, 0):
        bx = (x + k) % NX
        left0 = wgu[bx, :, 0].reshape(NZ * F, 2 * H)
        left1 = wgu[bx, :, 1].reshape(NZ * F, 2 * H)
        out = mm(left0, a01[0]) + mm(left1, a01[1])
        part[k] = out.astype(BF).reshape(NZ // NC, NC, F, ROWS)
        cp = remote(part.at[k, :, 1 - c], sib.at[k], s_sib.at[k], r_sib.at[k], sibling)
        cp.start()
        sib_copies[k] = cp
    for k in (2, 1, 3, 0):
        sib_copies[k].wait_recv()
        total = part[k, :, c].astype(F32) + sib[k].astype(F32)
        if k:
            xs[k] = total.astype(BF)
            cp = remote(xs.at[k], xr.at[k], s_x.at[k], r_x.at[k], dev((x + k) % NX, z, c, zh, y))
            cp.start()
            x_copies[k] = cp
        else:
            zs[...] = total

    hs[:, pl.ds(0, 2 * H)] = gg.T.astype(BF)
    hs[:, pl.ds(2 * H, H)] = pltpu.roll(hidden, CAP, 1).T.astype(BF)
    for q in range(NX):
        out = mm(ag[q].reshape(K, ROWS), hs[...])
        o_gate[pl.ds(q * K, K), :] = out[:, 0:H].astype(BF)
        o_up[pl.ds(q * K, K), :] = out[:, H : 2 * H].astype(BF)
        o_down[:, pl.ds(q * K, K)] = out[:, 2 * H :].T.astype(BF)

    for k in (1, 3, 2):
        x_copies[k].wait_recv()
        zs[...] += xr[k].astype(F32)
    half = zs[...].astype(BF)
    xs[0] = half

    def z_copy(q):
        return remote(
            xs.at[0, q], zr.at[z], s_z.at[q], r_z.at[z], dev(x, NC * q + c, c, zh, y)
        )

    for q in range(NZ // NC):
        @pl.when(NC * q + c != z)
        def _():
            z_copy(q).start()

    def back_place(h, k):
        return h * NY + k

    def back_copy(h, k, cc):
        to_h, to_y = (zh + h) % NH, (y + k) % NY
        return remote(
            back_s.at[h * NY + to_y], back_r.at[expert],
            s_back.at[(h * NY + k) * NC + cc], r_back.at[expert], dev(x, z, cc, to_h, to_y),
        )

    @pl.when(z % NC == c)
    def _():
        zr[z] = xs[0, z // NC]
        for k in range(1, NZ):
            bz = (z + k) % NZ
            remote(zr.at[bz], zr.at[bz], s_z.at[0], r_z.at[bz], sibling).wait_recv()
        total = jnp.sum(zr[...].astype(F32), axis=0).astype(BF)
        eye_f = (iota((ROWS, ROWS), 0) == iota((ROWS, ROWS), 1)).astype(BF)
        wide = jnp.concatenate([total, jnp.zeros((128 - F, ROWS), BF)], axis=0)
        rows = nt(eye_f, wide)
        back_s[...] = rows.astype(BF).reshape(E, 2 * CAP, 128)
        for h in reversed(range(NH)):
            for k in range(NY):
                if h or k:
                    for cc in range(NC):
                        back_copy(h, k, cc).start()
        remote(back_s.at[y], back_r.at[expert], s_back.at[0], r_back.at[expert], sibling).start()
        back_r[expert] = back_s[y]

    @pl.when(z % NC != c)
    def _():
        remote(back_s.at[y], back_r.at[expert], s_back.at[0], r_back.at[expert], sibling).wait_recv()

    for h in range(NH):
        for k in range(NY):
            if h or k:
                e2 = ((zh + h) % NH) * NY + (y + k) % NY
                remote(
                    back_s.at[0], back_r.at[e2], s_back.at[0], r_back.at[e2], sibling
                ).wait_recv()
    o_acts[...] = mm(combine, back_r[...].reshape(ROWS, 128))[:, 0:F].astype(BF)

    def z_sent(k, _):
        ag_copy(x, z, s_agz.at[k], sibling).wait_send()
        return 0

    lax.fori_loop(1, NZ, z_sent, 0)

    def x_sent(i, _):
        ag_copy(x, i % NZ, s_agx.at[i], sibling).wait_send()
        return 0

    lax.fori_loop(NZ, NX * NZ, x_sent, 0)

    def c_sent(i, _):
        ag_copy(x, z, s_agc.at[i], sibling).wait_send()
        return 0

    lax.fori_loop(0, NX * NZ, c_sent, 0)
    for cp in list(sib_copies.values()) + list(x_copies.values()):
        cp.wait_send()
    for q in range(NZ // NC):
        @pl.when(NC * q + c != z)
        def _():
            z_copy(q).wait_send()

    @pl.when(z % NC == c)
    def _():
        for h in range(NH):
            for k in range(NY):
                if h or k:
                    for cc in range(NC):
                        back_copy(h, k, cc).wait_send()
        remote(back_s.at[y], back_r.at[expert], s_back.at[0], r_back.at[expert], sibling).wait_send()


def body(acts, grad_out, routing, gates, w_gate, w_up, w_down):
    d = NX * K
    vm = pl.BlockSpec(memory_space=pltpu.VMEM)
    hbm = pl.BlockSpec(memory_space=pl.ANY)
    dma = pltpu.SemaphoreType.DMA
    out = pl.pallas_call(
        kernel,
        name="experts_backward",
        out_shape=(
            jax.ShapeDtypeStruct((d, H), BF),
            jax.ShapeDtypeStruct((d, H), BF),
            jax.ShapeDtypeStruct((H, d), BF),
            jax.ShapeDtypeStruct((T, F), BF),
        ),
        in_specs=[vm] * 4 + [hbm] * 3,
        out_specs=(vm,) * 4,
        scratch_shapes=[
            pltpu.VMEM((NX, NZ, NC, F, 2 * H), BF),
            pltpu.VMEM((NX, 3 * H, K), BF),
            pltpu.VMEM((E, 2 * CAP, 128), BF),
            pltpu.VMEM((E, 2 * CAP, 128), BF),
            pltpu.VMEM((NX, NZ, NC, F, ROWS), BF),
            pltpu.VMEM((3 * H, ROWS), F32),
            pltpu.VMEM((2, 2 * H, ROWS), BF),
            pltpu.VMEM((ROWS, 3 * H), BF),
            pltpu.VMEM((NX, NZ // NC, NC, F, ROWS), BF),
            pltpu.VMEM((NX, NZ // NC, F, ROWS), BF),
            pltpu.VMEM((NX, NZ // NC, F, ROWS), BF),
            pltpu.VMEM((NX, NZ // NC, F, ROWS), BF),
            pltpu.VMEM((NZ // NC, F, ROWS), F32),
            pltpu.VMEM((NZ, F, ROWS), BF),
            pltpu.VMEM((E, 2 * CAP, 128), BF),
            pltpu.VMEM((E, 2 * CAP, 128), BF),
            dma((2 + NX,)),
            dma((E,)),
            dma((E,)),
            dma((NX * NZ * NC,)),
            dma((NZ,)),
            dma((NX * NZ,)),
            dma((NX * NZ,)),
            dma((NX,)),
            dma((NX,)),
            dma((NX,)),
            dma((NX,)),
            dma((NZ // NC,)),
            dma((NZ,)),
            dma((E * NC,)),
            dma((E,)),
        ],
        compiler_params=pltpu.CompilerParams(
            collective_id=0, has_side_effects=True, vmem_limit_bytes=48 << 20
        ),
    )(
        acts,
        grad_out,
        routing,
        gates,
        w_gate.reshape(NX, NZ, NC, F, H),
        w_up.reshape(NX, NZ, NC, F, H),
        w_down.reshape(H, d),
    )
    return (out[0][None], out[1][None], out[2][None], out[3])


def solution(mesh):
    return jax.shard_map(
        body,
        mesh=mesh,
        in_specs=(
            P("expert", "tensor"),
            P("expert", "tensor"),
            P("expert", None),
            P("expert", None),
            P("expert", None, "tensor"),
            P("expert", None, "tensor"),
            P("expert", "tensor", None),
        ),
        out_specs=(
            P("expert", None, "tensor"),
            P("expert", None, "tensor"),
            P("expert", "tensor", None),
            P("expert", "tensor"),
        ),
        check_vma=False,
    )
```

```python
import jax
import jax.numpy as jnp
from jax import lax
from jax.experimental import pallas as pl
from jax.experimental.pallas import tpu as pltpu
from jax.sharding import PartitionSpec as P

NX, NZ, NC = 4, 8, 2
NH, NY = 2, 4
F = 48
T = 48
CAP = 24
E = NH * NY
ROWS = E * 2 * CAP
MSG = E * CAP
NQ = NZ // NC
HALF = NZ // 2
W = 256
G0 = 64
ZF = NZ * F
H = 128
K = NZ * NC * F
BF = jnp.bfloat16
F32 = jnp.float32
MESH = pl.DeviceIdType.MESH


def iota(shape, dim):
    return lax.broadcasted_iota(jnp.int32, shape, dim)


def split(i, per):
    q = (i * (65536 // per + 1)) >> 16
    return q, i - q * per


def mm(a, b):
    return jnp.dot(a, b, preferred_element_type=F32)


def nt(a, b):
    return lax.dot_general(a, b, (((1,), (1,)), ((), ())), preferred_element_type=F32)


def swap_z(rows):
    half = rows.shape[0] // 2
    return jnp.concatenate([rows[half:], rows[:half]], axis=0)


def kernel(
    acts_h, grad_h, routing_h, gates_h, wg, wu, wd,
    o_gate, o_up, o_down, o_acts,
    acts, grad, routing, gates,
    wall, w3, send, recv, ag, acc, aw, hs, part, sib, xs, xr, zs, zr, back_s, back_r,
    s_in, s_w, s_a2a, r_a2a, r_ag, s_agz, s_agx, s_agf, s_agc,
    s_sib, r_sib, s_x, r_x, s_z, r_z, s_back, r_back,
):
    tensor, expert = lax.axis_index("tensor"), lax.axis_index("expert")
    x, z, c = tensor // (NZ * NC), (tensor // NC) % NZ, tensor % NC
    zh, y = expert // NY, expert % NY
    z4 = (z + HALF) % NZ

    def dev(x_, z_, c_, zh_, y_):
        return ((x_ * NZ + z_) * NC + c_, zh_ * NY + y_)

    def remote(src, dst, ss, rs, to):
        return pltpu.make_async_remote_copy(
            src_ref=src, dst_ref=dst, send_sem=ss, recv_sem=rs, device_id=to, device_id_type=MESH
        )

    sibling = dev(x, z, 1 - c, zh, y)

    barrier = pltpu.get_barrier_semaphore()

    def greet(to):
        pl.semaphore_signal(barrier, inc=1, device_id=to, device_id_type=MESH)

    for k in range(NY):
        for cc in range(NC):
            greet(dev(x, z4, cc, 1 - zh, (y + k) % NY))
    for k in range(1, NZ):
        greet(dev(x, (z + k) % NZ, c, zh, y))
    for k in range(1, NY):
        for cc in range(NC):
            greet(dev(x, z, cc, zh, (y + k) % NY))
    for k in range(1, NX):
        greet(dev((x + k) % NX, z, c, zh, y))
    greet(sibling)

    in_copies = [
        pltpu.make_async_copy(a, b, s_in.at[i])
        for i, (a, b) in enumerate(
            [(routing_h, routing), (gates_h, gates), (acts_h, acts), (grad_h, grad)]
        )
    ]
    w_copies = [
        pltpu.make_async_copy(wg, wall.at[:, :, :, :, pl.ds(0, H)], s_w.at[0]),
        pltpu.make_async_copy(wu, wall.at[:, :, :, :, pl.ds(H, H)], s_w.at[1]),
        pltpu.make_async_copy(wd, o_down, s_w.at[2]),
    ]
    for cp in in_copies + w_copies:
        cp.start()
    for cp in in_copies:
        cp.wait()

    r = routing[...]
    g = gates[...]
    r0, r1 = r[0:1, :], r[1:2, :]
    names = iota((E, T), 0)
    c0, c1 = (r0 == names).astype(F32), (r1 == names).astype(F32)
    before = (iota((T, T), 0) < iota((T, T), 1)).astype(BF)
    earlier = mm((c0 + c1).astype(BF), before)
    pos0 = jnp.sum(earlier * c0, axis=0, keepdims=True)
    pos1 = jnp.sum((earlier + c0) * c1, axis=0, keepdims=True)
    key0 = jnp.where(pos0 < CAP, r0.astype(F32) * CAP + pos0, -1.0)
    key1 = jnp.where(pos1 < CAP, r1.astype(F32) * CAP + pos1, -1.0)
    want = iota((MSG, 1), 0).astype(F32)
    m0 = (want == key0).astype(F32)
    m1 = (want == key1).astype(F32)
    gate_slot = jnp.sum(m0 * g[0:1, :] + m1 * g[1:2, :], axis=1, keepdims=True)
    onehot = (m0 + m1).astype(BF)
    gap = jnp.zeros((MSG, G0 - F), F32)
    rows = jnp.concatenate(
        [mm(onehot, acts[...]), gap, mm(onehot, grad[...]) * gate_slot, gap], axis=1
    )
    send[...] = rows.astype(BF).reshape(E, CAP, 128)

    pl.semaphore_wait(barrier, 2 * NY + (NZ - 1) + 2 * (NY - 1) + (NX - 1) + 1)

    here = c * NY + y

    def far_copy(k):
        to_y = (y + k) % NY
        return remote(
            send.at[(1 - zh) * NY + to_y], recv.at[here], s_a2a.at[NY + k], r_a2a.at[here],
            dev(x, z4, 1, 1 - zh, to_y),
        )

    def near_copy(k):
        to_y = (y + k) % NY
        return remote(
            send.at[zh * NY + to_y], recv.at[here], s_a2a.at[k], r_a2a.at[here],
            dev(x, z, 0, zh, to_y),
        )

    own_copy = pltpu.make_async_copy(send.at[expert], recv.at[here], s_a2a.at[0])
    for k in range(NY):
        far_copy(k).start()
    for k in (2, 1, 3):
        near_copy(k).start()

    @pl.when(c == 0)
    def _():
        own_copy.start()

    @pl.when(c == 1)
    def _():
        near_copy(0).start()

    for cp in w_copies:
        cp.wait()
    for q in range(NX):
        wall[q, :, :, :, pl.ds(2 * H, H)] = o_down[:, pl.ds(q * K, K)].T.reshape(NZ, NC, F, H)
        for cc in range(NC):
            w3[q, cc] = wall[q, :, cc].reshape(ZF, 3 * H).T
    g_r, rest_r = split(iota((MSG, ROWS), 1), 2 * CAP)
    row = iota((MSG, ROWS), 0)
    pick = iota((F, 128), 1) - iota((F, 128), 0)
    put_x = (row == g_r * CAP + rest_r).astype(BF) * (rest_r < CAP).astype(BF)
    put_g = (row == g_r * CAP + rest_r - CAP).astype(BF) * (rest_r >= CAP).astype(BF)
    pick_x, pick_g = (pick == 0).astype(BF), (pick == G0).astype(BF)

    @pl.when(c == 0)
    def _():
        own_copy.wait()

    def a2a_arrived(i, _):
        @pl.when(jnp.logical_or(c == 1, i != here))
        def _():
            remote(recv.at[i], recv.at[i], s_a2a.at[0], r_a2a.at[i], sibling).wait_recv()

        return 0

    lax.fori_loop(0, E, a2a_arrived, 0)
    got = recv[...].reshape(MSG, 128)
    x_t, g_t = nt(pick_x, got).astype(BF), nt(pick_g, got).astype(BF)
    ag[x, z, c] = (mm(x_t, put_x) + mm(g_t, put_g)).astype(BF)

    left, right, far = (x + NX - 1) % NX, (x + 1) % NX, (x + 2) % NX

    def near_z(j):
        return z // HALF * HALF + (z + j) % HALF

    def ag_copy(bx, bz, ss, to):
        blk = ag.at[bx, bz, c]
        return remote(blk, blk, ss, r_ag.at[(bx * NZ + bz) * NC + c], to)

    def ag_arrived(bx, bz, bc):
        blk = ag.at[bx, bz, bc]
        remote(blk, blk, s_agz.at[0], r_ag.at[(bx * NZ + bz) * NC + bc], sibling).wait_recv()

    def hub_copy():
        return ag_copy(x, z, s_agz.at[0], dev(x, z4, c, zh, y))

    def local_copies(bz):
        i = 1 + (bz // HALF + z // HALF) % 2 * (HALF - 1)
        return [
            ag_copy(x, bz, s_agz.at[i + j - 1], dev(x, near_z(j), c, zh, y))
            for j in range(1, HALF)
        ]

    def to_other_core(bx, bz):
        return ag_copy(bx, bz, s_agc.at[bx * NZ + bz], sibling)

    def x_copies_of(bz):
        return [
            ag_copy(x, bz, s_agx.at[bz], dev(right, z, c, zh, y)),
            ag_copy(x, bz, s_agx.at[NZ + bz], dev(left, z, c, zh, y)),
        ]

    def forward_right(bz):
        return ag_copy(left, bz, s_agf.at[bz], dev(right, z, c, zh, y))

    def forward_left(bz):
        return ag_copy(right, bz, s_agf.at[bz], dev(left, z, c, zh, y))

    def spread(bz):
        for cp in x_copies_of(bz):
            cp.start()
        to_other_core(x, bz).start()

    def z_arrived(bz):
        ag_arrived(x, bz, c)
        spread(bz)

    def x_arrived(bz):
        ag_arrived(left, bz, c)

        @pl.when(bz % 2 == 0)
        def _():
            forward_right(bz).start()

        to_other_core(left, bz).start()
        ag_arrived(right, bz, c)

        @pl.when(bz % 2 == 1)
        def _():
            forward_left(bz).start()

        to_other_core(right, bz).start()

    def far_arrived(bz):
        ag_arrived(far, bz, c)
        to_other_core(far, bz).start()

    def loop(n, f):
        def step(j, _):
            f(j)
            return 0

        lax.fori_loop(1, n, step, 0)

    def over(j):
        return (near_z(j) + HALF) % NZ

    hub_copy().start()
    for cp in x_copies_of(z):
        cp.start()
    for cp in local_copies(z):
        cp.start()
    to_other_core(x, z).start()
    loop(HALF, lambda j: z_arrived(near_z(j)))
    x_arrived(z)
    ag_arrived(x, z4, c)
    for cp in local_copies(z4):
        cp.start()
    spread(z4)
    loop(HALF, lambda j: x_arrived(near_z(j)))
    far_arrived(z)
    loop(HALF, lambda j: z_arrived(over(j)))
    x_arrived(z4)
    loop(HALF, lambda j: far_arrived(near_z(j)))
    loop(HALF, lambda j: x_arrived(over(j)))
    far_arrived(z4)
    loop(HALF, lambda j: far_arrived(over(j)))

    def block_of(bx, h):
        rows = ag[bx, :, h].reshape(ZF, ROWS)
        return swap_z(rows) if h else rows

    for k in (0, 1, 3, 2):
        bx = (x + k) % NX

        def other_core(i, _):
            ag_arrived(bx, i, 1 - c)
            return 0

        lax.fori_loop(0, NZ, other_core, 0)
        for h in range(NH):
            rows = block_of(bx, h)
            for cc in range(NC):
                new = mm(w3[bx, cc], rows[:, cc * 128 : cc * 128 + W])
                if k:
                    acc[h, cc] += new
                else:
                    acc[h, cc] = new

    both = [acc[h, 0] + pltpu.roll(acc[h, 1], W - G0, 1) for h in range(NH)]
    pre = jnp.concatenate(both, axis=1)
    lane = iota((H, NH * W), 1) & (W - 1)
    is_x = jnp.logical_and(split(lane, 2 * CAP)[1] < CAP, lane < ROWS // 2)
    gate_pre, up_pre = pre[0:H], pre[H : 2 * H]
    grad_hidden = pltpu.roll(pre[2 * H :], NH * W - CAP, 1)
    sig = 1.0 / (1.0 + jnp.exp(-gate_pre))
    act = gate_pre * sig
    zero = jnp.zeros((H, NH * W), F32)
    hidden = jnp.where(is_x, act * up_pre, zero)
    gup = jnp.where(is_x, grad_hidden * act, zero)
    ggp = jnp.where(is_x, grad_hidden * up_pre * sig * (1.0 + gate_pre * (1.0 - sig)), zero)
    gg = jnp.concatenate([ggp, gup], axis=0)
    for h in range(NH):
        own = gg[:, h * W : (h + 1) * W]
        for cc in range(NC):
            shift = h * G0 + cc * CAP
            aw[h, pl.ds(cc * 2 * H, 2 * H), :] = (
                pltpu.roll(own, shift, 1) if shift else own
            ).astype(BF)

    sib_copies = {}
    for k in (2, 1, 3, 0):
        bx = (x + k) % NX
        lhs = jnp.concatenate(
            [wall[bx, :, cc, :, pl.ds(0, 2 * H)].reshape(ZF, 2 * H) for cc in range(NC)], axis=1
        )
        p0, p1 = mm(lhs, aw[0]), swap_z(mm(lhs, aw[1]))
        out = jnp.concatenate([p0[:, 0:128], p0[:, 128:] + p1[:, 0:128], p1[:, 128:]], axis=1)
        part[k] = out.astype(BF).reshape(NQ, NC, F, ROWS)
        cp = remote(part.at[k, :, 1 - c], sib.at[k], s_sib.at[k], r_sib.at[k], sibling)
        cp.start()
        sib_copies[k] = cp

    def turn(i):
        return (z // NC + NQ // 2 + i) % NQ

    def x_copy(k, q):
        return remote(
            xs.at[k, q], xr.at[k, q], s_x.at[k * NQ + q], r_x.at[k * NQ + q],
            dev((x + k) % NX, z, c, zh, y),
        )

    for k in (2, 1, 3, 0):
        sib_copies[k].wait_recv()
        total = part[k, :, c].astype(F32) + sib[k].astype(F32)
        if k:
            xs[k] = total.astype(BF)
        else:
            zs[...] = total
        if k == 2:
            for i in range(NQ):
                x_copy(k, turn(i)).start()
        if k == 3:
            for i in range(NQ):
                x_copy(1, turn(i)).start()
                x_copy(3, turn(i)).start()

    for h in range(NH):
        cols = slice(h * W, (h + 1) * W)
        own = jnp.concatenate([gg[:, cols], pltpu.roll(hidden[:, cols], CAP, 1)], axis=0)
        for cc in range(NC):
            hs[h, cc] = (pltpu.roll(own, G0, 1) if cc else own).T.astype(BF)

    def weight_grads(q):
        downs = []
        rows = [block_of(q, h) for h in range(NH)]
        for cc in range(NC):
            cols = slice(cc * 128, cc * 128 + W)
            out = mm(rows[0][:, cols], hs[0, cc]) + mm(rows[1][:, cols], hs[1, cc])
            out = out.astype(BF).reshape(NZ, F, 3 * H)
            o_gate[q, :, cc] = out[:, :, 0:H]
            o_up[q, :, cc] = out[:, :, H : 2 * H]
            downs.append(out[:, :, 2 * H :])
        o_down[:, pl.ds(q * K, K)] = jnp.stack(downs, axis=1).reshape(K, H).T

    def z_copy(q):
        return remote(xs.at[0, q], zr.at[z], s_z.at[q], r_z.at[z], dev(x, NC * q + c, c, zh, y))

    for i in range(NQ):
        weight_grads(i)
        q = turn(i)
        for k in (2, 1, 3):
            x_copy(k, q).wait_recv()
        total = zs[q] + xr[1, q].astype(F32) + xr[2, q].astype(F32) + xr[3, q].astype(F32)
        xs[0, q] = total.astype(BF)

        @pl.when(NC * q + c != z)
        def _():
            z_copy(q).start()

    def back_copy(h, k, cc):
        to_y = (y + k) % NY
        i = (h * NY + k) * NC + cc
        to = dev(x, z4, cc, 1 - zh, to_y) if h else dev(x, z, cc, zh, to_y)
        return remote(
            back_s.at[(h * NY + to_y) * NC + cc], back_r.at[expert],
            s_back.at[i], r_back.at[expert], to,
        )

    own_back = remote(
        back_s.at[y * NC + 1 - c], back_r.at[expert], s_back.at[0], r_back.at[expert], sibling
    )
    back_list = [(h, k, cc) for h in (1, 0) for k in range(NY) for cc in range(NC) if h or k]

    @pl.when(z % NC == c)
    def _():
        zr[z] = xs[0, z // NC]
        for k in range(1, NZ):
            bz = (z + k) % NZ
            remote(zr.at[bz], zr.at[bz], s_z.at[0], r_z.at[bz], sibling).wait_recv()
        total = jnp.sum(zr[...].astype(F32), axis=0).astype(BF)
        eye_f = (iota((ROWS, ROWS), 0) == iota((ROWS, ROWS), 1)).astype(BF)
        wide = jnp.concatenate([total, jnp.zeros((128 - F, ROWS), BF)], axis=0)
        back_s[...] = nt(eye_f, wide).astype(BF).reshape(E * NC, CAP, 128)
        for args in back_list:
            back_copy(*args).start()
        own_back.start()
        back_r[expert] = back_s[y * NC + c]

    eye = (iota((T, T), 0) == iota((T, T), 1)).astype(F32)

    def as_col(row):
        return jnp.sum(eye * row, axis=1, keepdims=True)

    want_r = iota((1, MSG), 1).astype(F32)
    combine = jnp.logical_or(want_r == as_col(key0), want_r == as_col(key1)).astype(BF)

    def back_arrived(i, _):
        @pl.when(jnp.logical_or(z % NC != c, i != expert))
        def _():
            remote(back_r.at[i], back_r.at[i], s_back.at[0], r_back.at[i], sibling).wait_recv()

        return 0

    lax.fori_loop(0, E, back_arrived, 0)
    o_acts[...] = mm(combine, back_r[...].reshape(MSG, 128))[:, 0:F].astype(BF)

    for k in range(NY):
        far_copy(k).wait_send()
    for k in range(1, NY):
        near_copy(k).wait_send()

    @pl.when(c == 1)
    def _():
        near_copy(0).wait_send()

    hub_copy().wait_send()
    for cp in local_copies(z) + local_copies(z4):
        cp.wait_send()

    def x_sent(i, _):
        for cp in x_copies_of(i):
            cp.wait_send()
        forward_right(i).wait_send()
        return 0

    lax.fori_loop(0, NZ, x_sent, 0)

    def c_sent(i, _):
        to_other_core(i // NZ, i % NZ).wait_send()
        return 0

    lax.fori_loop(0, NX * NZ, c_sent, 0)
    for cp in sib_copies.values():
        cp.wait_send()
    for k in range(1, NX):
        for q in range(NQ):
            x_copy(k, q).wait_send()
    for q in range(NQ):
        @pl.when(NC * q + c != z)
        def _():
            z_copy(q).wait_send()

    @pl.when(z % NC == c)
    def _():
        for args in back_list:
            back_copy(*args).wait_send()
        own_back.wait_send()


def put(*refs):
    n = len(refs) // 2
    sems = refs[-1]
    copies = [pltpu.make_async_copy(refs[i], refs[n + i], sems.at[i]) for i in range(n)]
    for cp in copies:
        cp.start()
    for cp in copies:
        cp.wait()


def body(acts, grad_out, routing, gates, w_gate, w_up, w_down):
    d = NX * K
    vm = pl.BlockSpec(memory_space=pltpu.VMEM)
    hbm = pl.BlockSpec(memory_space=pltpu.HBM)
    dma = pltpu.SemaphoreType.DMA
    shapes = (
        jax.ShapeDtypeStruct((NX, NZ, NC, F, H), BF),
        jax.ShapeDtypeStruct((NX, NZ, NC, F, H), BF),
        jax.ShapeDtypeStruct((H, d), BF),
        jax.ShapeDtypeStruct((T, F), BF),
    )
    out = pl.pallas_call(
        kernel,
        name="experts_backward",
        out_shape=shapes,
        in_specs=[hbm] * 7,
        out_specs=(vm,) * 4,
        scratch_shapes=[
            pltpu.VMEM((T, F), BF),
            pltpu.VMEM((T, F), BF),
            pltpu.VMEM((2, T), jnp.int32),
            pltpu.VMEM((2, T), F32),
            pltpu.VMEM((NX, NZ, NC, F, 3 * H), BF),
            pltpu.VMEM((NX, NC, 3 * H, ZF), BF),
            pltpu.VMEM((E, CAP, 128), BF),
            pltpu.VMEM((E, CAP, 128), BF),
            pltpu.VMEM((NX, NZ, NC, F, ROWS), BF),
            pltpu.VMEM((NH, NC, 3 * H, W), F32),
            pltpu.VMEM((NH, NC * 2 * H, W), BF),
            pltpu.VMEM((NH, NC, W, 3 * H), BF),
            pltpu.VMEM((NX, NQ, NC, F, ROWS), BF),
            pltpu.VMEM((NX, NQ, F, ROWS), BF),
            pltpu.VMEM((NX, NQ, F, ROWS), BF),
            pltpu.VMEM((NX, NQ, F, ROWS), BF),
            pltpu.VMEM((NQ, F, ROWS), F32),
            pltpu.VMEM((NZ, F, ROWS), BF),
            pltpu.VMEM((E * NC, CAP, 128), BF),
            pltpu.VMEM((E, CAP, 128), BF),
            dma((4,)),
            dma((3,)),
            dma((E,)),
            dma((E,)),
            dma((NX * NZ * NC,)),
            dma((2 * HALF - 1,)),
            dma((2 * NZ,)),
            dma((NZ,)),
            dma((NX * NZ,)),
            dma((NX,)),
            dma((NX,)),
            dma((NX * NQ,)),
            dma((NX * NQ,)),
            dma((NQ,)),
            dma((NZ,)),
            dma((E * NC,)),
            dma((E,)),
        ],
        compiler_params=pltpu.CompilerParams(
            collective_id=0, has_side_effects=True, vmem_limit_bytes=40 << 20
        ),
    )(
        *[
            pltpu.with_memory_space_constraint(a, pltpu.HBM)
            for a in (
                acts,
                grad_out,
                routing.T,
                gates.T,
                w_gate.reshape(NX, NZ, NC, F, H),
                w_up.reshape(NX, NZ, NC, F, H),
                w_down.reshape(H, d),
            )
        ]
    )
    shapes = (jax.ShapeDtypeStruct((d, H), BF),) * 2 + shapes[2:]
    out = pl.pallas_call(
        put,
        name="put",
        out_shape=shapes,
        in_specs=[pl.BlockSpec(memory_space=pl.ANY)] * 4,
        out_specs=(hbm,) * 4,
        scratch_shapes=[dma((4,))],
        compiler_params=pltpu.CompilerParams(vmem_limit_bytes=1 << 20),
    )(out[0].reshape(d, H), out[1].reshape(d, H), out[2], out[3])
    return (out[0][None], out[1][None], out[2][None], out[3])


def solution(mesh):
    return jax.shard_map(
        body,
        mesh=mesh,
        in_specs=(
            P("expert", "tensor"),
            P("expert", "tensor"),
            P("expert", None),
            P("expert", None),
            P("expert", None, "tensor"),
            P("expert", None, "tensor"),
            P("expert", "tensor", None),
        ),
        out_specs=(
            P("expert", None, "tensor"),
            P("expert", None, "tensor"),
            P("expert", "tensor", None),
            P("expert", "tensor"),
        ),
        check_vma=False,
    )
```

```python
import jax
import jax.numpy as jnp
from jax import lax
from jax.experimental import pallas as pl
from jax.experimental.pallas import tpu as pltpu
from jax.sharding import PartitionSpec as P

NX, NZ, NC = 4, 8, 2
NH, NY = 2, 4
F = 48
T = 48
CAP = 24
E = NH * NY
ROWS = E * 2 * CAP
MSG = E * CAP
NQ = NZ // NC
HALF = NZ // 2
W = 256
G0 = 64
ZF = NZ * F
PARTS = ((128, 256), (0, 128))
H = 128
K = NZ * NC * F
BF = jnp.bfloat16
F32 = jnp.float32
MESH = pl.DeviceIdType.MESH


def iota(shape, dim):
    return lax.broadcasted_iota(jnp.int32, shape, dim)


def split(i, per):
    q = (i * (65536 // per + 1)) >> 16
    return q, i - q * per


def mm(a, b):
    return jnp.dot(a, b, preferred_element_type=F32)


def nt(a, b):
    return lax.dot_general(a, b, (((1,), (1,)), ((), ())), preferred_element_type=F32)


def swap_z(rows):
    half = rows.shape[0] // 2
    return jnp.concatenate([rows[half:], rows[:half]], axis=0)


def kernel(
    acts_h, grad_h, routing_h, gates_h, wg, wu, wd,
    o_gate, o_up, o_down, o_acts,
    acts, grad, routing, gates,
    wall, w3, send, recv, ag, acc, aw, hs, part, sib, xs, xr, zs, zr, back_s, back_r,
    s_in, s_w, s_a2a, r_a2a, r_ag, s_agz, s_agx, s_agf, s_agc,
    s_sib, r_sib, s_x, r_x, s_z, r_z, s_back, r_back,
):
    tensor, expert = lax.axis_index("tensor"), lax.axis_index("expert")
    x, z, c = tensor // (NZ * NC), (tensor // NC) % NZ, tensor % NC
    zh, y = expert // NY, expert % NY
    z4 = (z + HALF) % NZ

    def dev(x_, z_, c_, zh_, y_):
        return ((x_ * NZ + z_) * NC + c_, zh_ * NY + y_)

    def remote(src, dst, ss, rs, to):
        return pltpu.make_async_remote_copy(
            src_ref=src, dst_ref=dst, send_sem=ss, recv_sem=rs, device_id=to, device_id_type=MESH
        )

    sibling = dev(x, z, 1 - c, zh, y)

    barrier = pltpu.get_barrier_semaphore()

    def greet(to):
        pl.semaphore_signal(barrier, inc=1, device_id=to, device_id_type=MESH)

    for k in range(NY):
        for cc in range(NC):
            greet(dev(x, z4, cc, 1 - zh, (y + k) % NY))
    for k in range(1, NZ):
        greet(dev(x, (z + k) % NZ, c, zh, y))
    for k in range(1, NY):
        for cc in range(NC):
            greet(dev(x, z, cc, zh, (y + k) % NY))
    for k in range(1, NX):
        greet(dev((x + k) % NX, z, c, zh, y))
    greet(sibling)

    in_copies = [
        pltpu.make_async_copy(a, b, s_in.at[i])
        for i, (a, b) in enumerate(
            [(routing_h, routing), (gates_h, gates), (acts_h, acts), (grad_h, grad)]
        )
    ]
    w_copies = [
        pltpu.make_async_copy(wg, wall.at[:, :, :, :, pl.ds(0, H)], s_w.at[0]),
        pltpu.make_async_copy(wu, wall.at[:, :, :, :, pl.ds(H, H)], s_w.at[1]),
        pltpu.make_async_copy(wd, o_down, s_w.at[2]),
    ]
    for cp in in_copies + w_copies:
        cp.start()
    for cp in in_copies:
        cp.wait()

    r = routing[...]
    g = gates[...]
    r0, r1 = r[0:1, :], r[1:2, :]
    names = iota((E, T), 0)
    c0, c1 = (r0 == names).astype(F32), (r1 == names).astype(F32)
    before = (iota((T, T), 0) < iota((T, T), 1)).astype(BF)
    earlier = mm((c0 + c1).astype(BF), before)
    pos0 = jnp.sum(earlier * c0, axis=0, keepdims=True)
    pos1 = jnp.sum((earlier + c0) * c1, axis=0, keepdims=True)
    key0 = jnp.where(pos0 < CAP, r0.astype(F32) * CAP + pos0, -1.0)
    key1 = jnp.where(pos1 < CAP, r1.astype(F32) * CAP + pos1, -1.0)
    want = iota((MSG, 1), 0).astype(F32)
    m0 = (want == key0).astype(F32)
    m1 = (want == key1).astype(F32)
    gate_slot = jnp.sum(m0 * g[0:1, :] + m1 * g[1:2, :], axis=1, keepdims=True)
    onehot = (m0 + m1).astype(BF)
    gap = jnp.zeros((MSG, G0 - F), F32)
    rows = jnp.concatenate(
        [mm(onehot, acts[...]), gap, mm(onehot, grad[...]) * gate_slot, gap], axis=1
    )
    send[...] = rows.astype(BF).reshape(E, CAP, 128)

    pl.semaphore_wait(barrier, 2 * NY + (NZ - 1) + 2 * (NY - 1) + (NX - 1) + 1)

    unsent = []

    def finish():
        for f in unsent:
            f()

    here = c * NY + y

    def far_copy(k):
        to_y = (y + k) % NY
        return remote(
            send.at[(1 - zh) * NY + to_y], recv.at[here], s_a2a.at[NY + k], r_a2a.at[here],
            dev(x, z4, 1, 1 - zh, to_y),
        )

    def near_copy(k):
        to_y = (y + k) % NY
        return remote(
            send.at[zh * NY + to_y], recv.at[here], s_a2a.at[k], r_a2a.at[here],
            dev(x, z, 0, zh, to_y),
        )

    own_copy = pltpu.make_async_copy(send.at[expert], recv.at[here], s_a2a.at[0])
    for k in range(NY):
        far_copy(k).start()
    for k in (2, 1, 3):
        near_copy(k).start()

    @pl.when(c == 0)
    def _():
        own_copy.start()

    @pl.when(c == 1)
    def _():
        near_copy(0).start()

    def a2a_sent():
        for k in range(NY):
            far_copy(k).wait_send()
        for k in range(1, NY):
            near_copy(k).wait_send()

        @pl.when(c == 1)
        def _():
            near_copy(0).wait_send()

    unsent.append(a2a_sent)

    for cp in w_copies:
        cp.wait()
    for q in range(NX):
        wall[q, :, :, :, pl.ds(2 * H, H)] = o_down[:, pl.ds(q * K, K)].T.reshape(NZ, NC, F, H)
        for cc in range(NC):
            w3[q, cc] = wall[q, :, cc].reshape(ZF, 3 * H).T
    g_r, rest_r = split(iota((MSG, ROWS), 1), 2 * CAP)
    row = iota((MSG, ROWS), 0)
    pick = iota((F, 128), 1) - iota((F, 128), 0)
    put_x = (row == g_r * CAP + rest_r).astype(BF) * (rest_r < CAP).astype(BF)
    put_g = (row == g_r * CAP + rest_r - CAP).astype(BF) * (rest_r >= CAP).astype(BF)
    pick_x, pick_g = (pick == 0).astype(BF), (pick == G0).astype(BF)

    @pl.when(c == 0)
    def _():
        own_copy.wait()

    def a2a_arrived(i, _):
        @pl.when(jnp.logical_or(c == 1, i != here))
        def _():
            remote(recv.at[i], recv.at[i], s_a2a.at[0], r_a2a.at[i], sibling).wait_recv()

        return 0

    lax.fori_loop(0, E, a2a_arrived, 0)
    got = recv[...].reshape(MSG, 128)
    x_t, g_t = nt(pick_x, got).astype(BF), nt(pick_g, got).astype(BF)
    ag[x, z, c] = (mm(x_t, put_x) + mm(g_t, put_g)).astype(BF)

    left, right, far = (x + NX - 1) % NX, (x + 1) % NX, (x + 2) % NX

    def near_z(j):
        return z // HALF * HALF + (z + j) % HALF

    def ag_copy(bx, bz, ss, to):
        blk = ag.at[bx, bz, c]
        return remote(blk, blk, ss, r_ag.at[(bx * NZ + bz) * NC + c], to)

    def ag_arrived(bx, bz, bc):
        blk = ag.at[bx, bz, bc]
        remote(blk, blk, s_agz.at[0], r_ag.at[(bx * NZ + bz) * NC + bc], sibling).wait_recv()

    def hub_copy():
        return ag_copy(x, z, s_agz.at[0], dev(x, z4, c, zh, y))

    def local_copies(bz):
        i = 1 + (bz // HALF + z // HALF) % 2 * (HALF - 1)
        return [
            ag_copy(x, bz, s_agz.at[i + j - 1], dev(x, near_z(j), c, zh, y))
            for j in range(1, HALF)
        ]

    def to_other_core(bx, bz):
        return ag_copy(bx, bz, s_agc.at[bx * NZ + bz], sibling)

    def x_copies_of(bz):
        return [
            ag_copy(x, bz, s_agx.at[bz], dev(right, z, c, zh, y)),
            ag_copy(x, bz, s_agx.at[NZ + bz], dev(left, z, c, zh, y)),
        ]

    def forward_right(bz):
        return ag_copy(left, bz, s_agf.at[bz], dev(right, z, c, zh, y))

    def forward_left(bz):
        return ag_copy(right, bz, s_agf.at[bz], dev(left, z, c, zh, y))

    def unicast(bz):
        return bz // HALF != z // HALF

    def spread(bz):
        @pl.when(unicast(bz))
        def _():
            ag_copy(x, bz, s_agf.at[bz], dev(far, z, c, zh, y)).start()

        for cp in x_copies_of(bz):
            cp.start()
        to_other_core(x, bz).start()

    def z_arrived(bz):
        ag_arrived(x, bz, c)
        spread(bz)

    def x_arrived(bz):
        ag_arrived(left, bz, c)

        @pl.when(jnp.logical_and(bz % 2 == 0, jnp.logical_not(unicast(bz))))
        def _():
            forward_right(bz).start()

        to_other_core(left, bz).start()
        ag_arrived(right, bz, c)

        @pl.when(jnp.logical_and(bz % 2 == 1, jnp.logical_not(unicast(bz))))
        def _():
            forward_left(bz).start()

        to_other_core(right, bz).start()

    def far_arrived(bz):
        ag_arrived(far, bz, c)
        to_other_core(far, bz).start()

    def loop(n, f):
        def step(j, _):
            f(j)
            return 0

        lax.fori_loop(1, n, step, 0)

    def over(j):
        return (near_z(j) + HALF) % NZ

    hub_copy().start()
    for cp in x_copies_of(z):
        cp.start()
    for cp in local_copies(z):
        cp.start()
    to_other_core(x, z).start()
    loop(HALF, lambda j: z_arrived(near_z(j)))
    x_arrived(z)
    ag_arrived(x, z4, c)
    for cp in local_copies(z4):
        cp.start()
    spread(z4)
    loop(HALF, lambda j: x_arrived(near_z(j)))
    far_arrived(z)
    loop(HALF, lambda j: z_arrived(over(j)))
    x_arrived(z4)
    loop(HALF, lambda j: far_arrived(near_z(j)))
    loop(HALF, lambda j: x_arrived(over(j)))
    far_arrived(z4)
    loop(HALF, lambda j: far_arrived(over(j)))

    def gather_sent():
        hub_copy().wait_send()
        for cp in local_copies(z) + local_copies(z4):
            cp.wait_send()

        def x_sent(i, _):
            for cp in x_copies_of(i):
                cp.wait_send()
            forward_right(i).wait_send()
            return 0

        lax.fori_loop(0, NZ, x_sent, 0)

        def c_sent(i, _):
            to_other_core(i // NZ, i % NZ).wait_send()
            return 0

        lax.fori_loop(0, NX * NZ, c_sent, 0)

    unsent.append(gather_sent)
    def block_of(bx, h):
        rows = ag[bx, :, h].reshape(ZF, ROWS)
        return swap_z(rows) if h else rows

    for k in (0, 1, 3, 2):
        bx = (x + k) % NX

        def other_core(i, _):
            ag_arrived(bx, i, 1 - c)
            return 0

        lax.fori_loop(0, NZ, other_core, 0)
        for h in range(NH):
            rows = block_of(bx, h)
            for cc in range(NC):
                new = mm(w3[bx, cc], rows[:, cc * 128 : cc * 128 + W])
                if k:
                    acc[h, cc] += new
                else:
                    acc[h, cc] = new

    both = [acc[h, 0] + pltpu.roll(acc[h, 1], W - G0, 1) for h in range(NH)]
    pre = jnp.concatenate(both, axis=1)
    lane = iota((H, NH * W), 1) & (W - 1)
    is_x = jnp.logical_and(split(lane, 2 * CAP)[1] < CAP, lane < ROWS // 2)
    gate_pre, up_pre = pre[0:H], pre[H : 2 * H]
    grad_hidden = pltpu.roll(pre[2 * H :], NH * W - CAP, 1)
    sig = 1.0 / (1.0 + jnp.exp(-gate_pre))
    act = gate_pre * sig
    zero = jnp.zeros((H, NH * W), F32)
    hidden = jnp.where(is_x, act * up_pre, zero)
    gup = jnp.where(is_x, grad_hidden * act, zero)
    ggp = jnp.where(is_x, grad_hidden * up_pre * sig * (1.0 + gate_pre * (1.0 - sig)), zero)
    gg = jnp.concatenate([ggp, gup], axis=0)
    for h in range(NH):
        own = gg[:, h * W : (h + 1) * W]
        for cc in range(NC):
            shift = h * G0 + cc * CAP
            aw[h, pl.ds(cc * 2 * H, 2 * H), :] = (
                pltpu.roll(own, shift, 1) if shift else own
            ).astype(BF)

    sib_copies = {}
    for k in (2, 1, 3, 0):
        bx = (x + k) % NX
        lhs = jnp.concatenate(
            [wall[bx, :, cc, :, pl.ds(0, 2 * H)].reshape(ZF, 2 * H) for cc in range(NC)], axis=1
        )
        p0, p1 = mm(lhs, aw[0]), swap_z(mm(lhs, aw[1]))
        out = jnp.concatenate([p0[:, 0:128], p0[:, 128:] + p1[:, 0:128], p1[:, 128:]], axis=1)
        part[k] = out.astype(BF).reshape(NQ, NC, F, ROWS)
        cp = remote(part.at[k, :, 1 - c], sib.at[k], s_sib.at[k], r_sib.at[k], sibling)
        cp.start()
        sib_copies[k] = cp

    unsent.append(lambda: [cp.wait_send() for cp in sib_copies.values()])
    def turn(i):
        pair, lower = z // NC, 1 - z // HALF
        if i < NQ // 2:
            return lower * (NQ - 1 - i) + (1 - lower) * i
        return pair if i == NQ - 1 else lower * (1 - pair) + (1 - lower) * (NQ + 1 - pair)

    def cols(p):
        return pl.ds(*PARTS[p])

    def x_copy(k, q, p):
        i = (p * NX + k) * NQ + q
        return remote(
            xs.at[k, q, :, cols(p)], xr.at[k, q, :, cols(p)], s_x.at[i], r_x.at[i],
            dev((x + k) % NX, z, c, zh, y),
        )

    for k in (2, 1, 3, 0):
        sib_copies[k].wait_recv()
        total = part[k, :, c].astype(F32) + sib[k].astype(F32)
        if k:
            xs[k] = total.astype(BF)
            x_copy(k, turn(0), 0).start()
        else:
            zs[...] = total
        if k == 3:
            for p in range(2):
                for i in range(1 - p, NQ):
                    for kk in (2, 1, 3):
                        x_copy(kk, turn(i), p).start()

    def x_left():
        for k in range(1, NX):
            for q in range(NQ):
                for p in range(2):
                    x_copy(k, q, p).wait_send()

    unsent.append(x_left)

    for h in range(NH):
        cut = slice(h * W, (h + 1) * W)
        own = jnp.concatenate([gg[:, cut], pltpu.roll(hidden[:, cut], CAP, 1)], axis=0)
        for cc in range(NC):
            hs[h, cc] = (pltpu.roll(own, G0, 1) if cc else own).T.astype(BF)

    def weight_grads(q):
        downs = []
        rows = [block_of(q, h) for h in range(NH)]
        for cc in range(NC):
            cut = slice(cc * 128, cc * 128 + W)
            out = mm(rows[0][:, cut], hs[0, cc]) + mm(rows[1][:, cut], hs[1, cc])
            out = out.astype(BF).reshape(NZ, F, 3 * H)
            o_gate[q, :, cc] = out[:, :, 0:H]
            o_up[q, :, cc] = out[:, :, H : 2 * H]
            downs.append(out[:, :, 2 * H :])
        o_down[:, pl.ds(q * K, K)] = jnp.stack(downs, axis=1).reshape(K, H).T

    def z_copy(q, p):
        return remote(
            xs.at[0, q, :, cols(p)], zr.at[z, :, cols(p)], s_z.at[p * NQ + q],
            r_z.at[p * NZ + z], dev(x, NC * q + c, c, zh, y),
        )

    for p in range(2):
        for i in range(NQ):
            if p == 0:
                weight_grads(i)
            q = turn(i)
            for k in (2, 1, 3):
                x_copy(k, q, p).wait_recv()
            total = zs[q, :, cols(p)]
            for k in (1, 2, 3):
                total += xr[k, q, :, cols(p)].astype(F32)
            xs[0, q, :, cols(p)] = total.astype(BF)

            @pl.when(NC * q + c != z)
            def _():
                z_copy(q, p).start()

    def z_sent():
        for q in range(NQ):
            @pl.when(NC * q + c != z)
            def _():
                for p in range(2):
                    z_copy(q, p).wait_send()

    unsent.append(z_sent)
    def back_copy(h, k, cc):
        to_y = (y + k) % NY
        i = (h * NY + k) * NC + cc
        to = dev(x, z4, cc, 1 - zh, to_y) if h else dev(x, z, cc, zh, to_y)
        return remote(
            back_s.at[(h * NY + to_y) * NC + cc], back_r.at[expert],
            s_back.at[i], r_back.at[expert], to,
        )

    own_back = remote(
        back_s.at[y * NC + 1 - c], back_r.at[expert], s_back.at[0], r_back.at[expert], sibling
    )
    back_list = [(h, k, cc) for h in (1, 0) for k in range(NY) for cc in range(NC) if h or k]

    @pl.when(z % NC == c)
    def _():
        eye_f = (iota((W, W), 0) == iota((W, W), 1)).astype(BF)
        for p in range(2):
            zr[z, :, cols(p)] = xs[0, z // NC, :, cols(p)]
            for k in range(1, NZ):
                bz = (z + k) % NZ
                blk = zr.at[bz, :, cols(p)]
                remote(blk, blk, s_z.at[0], r_z.at[p * NZ + bz], sibling).wait_recv()
            h = 1 - p
            total = jnp.sum(zr[:, :, h * 128 : h * 128 + W].astype(F32), axis=0).astype(BF)
            wide = jnp.concatenate([total, jnp.zeros((128 - F, W), BF)], axis=0)
            rows = nt(eye_f, wide)[h * G0 : h * G0 + MSG]
            back_s[h * E : (h + 1) * E] = rows.astype(BF).reshape(E, CAP, 128)
            for args in back_list:
                if args[0] == h:
                    back_copy(*args).start()
        own_back.start()
        back_r[expert] = back_s[y * NC + c]

    def back_sent():
        @pl.when(z % NC == c)
        def _():
            for args in back_list:
                back_copy(*args).wait_send()
            own_back.wait_send()

    unsent.append(back_sent)

    eye = (iota((T, T), 0) == iota((T, T), 1)).astype(F32)

    def as_col(row):
        return jnp.sum(eye * row, axis=1, keepdims=True)

    want_r = iota((1, MSG), 1).astype(F32)
    combine = jnp.logical_or(want_r == as_col(key0), want_r == as_col(key1)).astype(BF)

    def back_arrived(i, _):
        @pl.when(jnp.logical_or(z % NC != c, i != expert))
        def _():
            remote(back_r.at[i], back_r.at[i], s_back.at[0], r_back.at[i], sibling).wait_recv()

        return 0

    lax.fori_loop(0, E, back_arrived, 0)
    o_acts[...] = mm(combine, back_r[...].reshape(MSG, 128))[:, 0:F].astype(BF)

    finish()


def put(*refs):
    n = len(refs) // 2
    sems = refs[-1]
    copies = [pltpu.make_async_copy(refs[i], refs[n + i], sems.at[i]) for i in range(n)]
    for cp in copies:
        cp.start()
    for cp in copies:
        cp.wait()


def body(acts, grad_out, routing, gates, w_gate, w_up, w_down):
    d = NX * K
    vm = pl.BlockSpec(memory_space=pltpu.VMEM)
    hbm = pl.BlockSpec(memory_space=pltpu.HBM)
    dma = pltpu.SemaphoreType.DMA
    shapes = (
        jax.ShapeDtypeStruct((NX, NZ, NC, F, H), BF),
        jax.ShapeDtypeStruct((NX, NZ, NC, F, H), BF),
        jax.ShapeDtypeStruct((H, d), BF),
        jax.ShapeDtypeStruct((T, F), BF),
    )
    out = pl.pallas_call(
        kernel,
        name="experts_backward",
        out_shape=shapes,
        in_specs=[hbm] * 7,
        out_specs=(vm,) * 4,
        scratch_shapes=[
            pltpu.VMEM((T, F), BF),
            pltpu.VMEM((T, F), BF),
            pltpu.VMEM((2, T), jnp.int32),
            pltpu.VMEM((2, T), F32),
            pltpu.VMEM((NX, NZ, NC, F, 3 * H), BF),
            pltpu.VMEM((NX, NC, 3 * H, ZF), BF),
            pltpu.VMEM((E, CAP, 128), BF),
            pltpu.VMEM((E, CAP, 128), BF),
            pltpu.VMEM((NX, NZ, NC, F, ROWS), BF),
            pltpu.VMEM((NH, NC, 3 * H, W), F32),
            pltpu.VMEM((NH, NC * 2 * H, W), BF),
            pltpu.VMEM((NH, NC, W, 3 * H), BF),
            pltpu.VMEM((NX, NQ, NC, F, ROWS), BF),
            pltpu.VMEM((NX, NQ, F, ROWS), BF),
            pltpu.VMEM((NX, NQ, F, ROWS), BF),
            pltpu.VMEM((NX, NQ, F, ROWS), BF),
            pltpu.VMEM((NQ, F, ROWS), F32),
            pltpu.VMEM((NZ, F, ROWS), BF),
            pltpu.VMEM((E * NC, CAP, 128), BF),
            pltpu.VMEM((E, CAP, 128), BF),
            dma((4,)),
            dma((3,)),
            dma((E,)),
            dma((E,)),
            dma((NX * NZ * NC,)),
            dma((2 * HALF - 1,)),
            dma((2 * NZ,)),
            dma((NZ,)),
            dma((NX * NZ,)),
            dma((NX,)),
            dma((NX,)),
            dma((2 * NX * NQ,)),
            dma((2 * NX * NQ,)),
            dma((2 * NQ,)),
            dma((2 * NZ,)),
            dma((E * NC,)),
            dma((E,)),
        ],
        compiler_params=pltpu.CompilerParams(
            collective_id=0, has_side_effects=True, vmem_limit_bytes=40 << 20
        ),
    )(
        *[
            pltpu.with_memory_space_constraint(a, pltpu.HBM)
            for a in (
                acts,
                grad_out,
                routing.T,
                gates.T,
                w_gate.reshape(NX, NZ, NC, F, H),
                w_up.reshape(NX, NZ, NC, F, H),
                w_down.reshape(H, d),
            )
        ]
    )
    shapes = (jax.ShapeDtypeStruct((d, H), BF),) * 2 + shapes[2:]
    out = pl.pallas_call(
        put,
        name="put",
        out_shape=shapes,
        in_specs=[pl.BlockSpec(memory_space=pl.ANY)] * 4,
        out_specs=(hbm,) * 4,
        scratch_shapes=[dma((4,))],
        compiler_params=pltpu.CompilerParams(vmem_limit_bytes=1 << 20),
    )(out[0].reshape(d, H), out[1].reshape(d, H), out[2], out[3])
    return (out[0][None], out[1][None], out[2][None], out[3])


def solution(mesh):
    return jax.shard_map(
        body,
        mesh=mesh,
        in_specs=(
            P("expert", "tensor"),
            P("expert", "tensor"),
            P("expert", None),
            P("expert", None),
            P("expert", None, "tensor"),
            P("expert", None, "tensor"),
            P("expert", "tensor", None),
        ),
        out_specs=(
            P("expert", None, "tensor"),
            P("expert", None, "tensor"),
            P("expert", "tensor", None),
            P("expert", "tensor"),
        ),
        check_vma=False,
    )
```

```python
import jax
import jax.numpy as jnp
from jax import lax
from jax.experimental import pallas as pl
from jax.experimental.pallas import tpu as pltpu
from jax.sharding import PartitionSpec as P

NX, NZ, NC = 4, 8, 2
NH, NY = 2, 4
F = 48
T = 48
CAP = 24
E = NH * NY
ROWS = E * 2 * CAP
MSG = E * CAP
NQ = NZ // NC
HALF = NZ // 2
W = 256
G0 = 64
ZF = NZ * F
PARTS = ((128, 256), (0, 128))
H = 128
K = NZ * NC * F
BF = jnp.bfloat16
F32 = jnp.float32
MESH = pl.DeviceIdType.MESH


def iota(shape, dim):
    return lax.broadcasted_iota(jnp.int32, shape, dim)


def split(i, per):
    q = (i * (65536 // per + 1)) >> 16
    return q, i - q * per


def mm(a, b):
    return jnp.dot(a, b, preferred_element_type=F32)


def nt(a, b):
    return lax.dot_general(a, b, (((1,), (1,)), ((), ())), preferred_element_type=F32)


def swap_z(rows):
    half = rows.shape[0] // 2
    return jnp.concatenate([rows[half:], rows[:half]], axis=0)


def kernel(
    acts_h, grad_h, routing_h, gates_h, wg, wu, wd,
    o_gate, o_up, o_down, o_acts,
    acts, grad, routing, gates,
    wall, w3, send, recv, ag, acc, aw, hs, part, sib, xs, xr, zs, zr, back_s, back_r,
    s_in, s_w, s_a2a, r_a2a, r_ag, s_agz, s_agx, s_agf, s_agc,
    s_sib, r_sib, s_x, r_x, s_z, r_z, s_back, r_back,
):
    tensor, expert = lax.axis_index("tensor"), lax.axis_index("expert")
    x, z, c = tensor // (NZ * NC), (tensor // NC) % NZ, tensor % NC
    zh, y = expert // NY, expert % NY
    z4 = (z + HALF) % NZ

    def dev(x_, z_, c_, zh_, y_):
        return ((x_ * NZ + z_) * NC + c_, zh_ * NY + y_)

    def remote(src, dst, ss, rs, to):
        return pltpu.make_async_remote_copy(
            src_ref=src, dst_ref=dst, send_sem=ss, recv_sem=rs, device_id=to, device_id_type=MESH
        )

    sibling = dev(x, z, 1 - c, zh, y)

    barrier = pltpu.get_barrier_semaphore()

    def greet(to):
        pl.semaphore_signal(barrier, inc=1, device_id=to, device_id_type=MESH)

    for k in range(NY):
        for cc in range(NC):
            greet(dev(x, z4, cc, 1 - zh, (y + k) % NY))
    for k in range(1, NZ):
        greet(dev(x, (z + k) % NZ, c, zh, y))
    for k in range(1, NY):
        for cc in range(NC):
            greet(dev(x, z, cc, zh, (y + k) % NY))
    for k in range(1, NX):
        greet(dev((x + k) % NX, z, c, zh, y))
    greet(sibling)

    in_copies = [
        pltpu.make_async_copy(a, b, s_in.at[i])
        for i, (a, b) in enumerate(
            [(routing_h, routing), (gates_h, gates), (acts_h, acts), (grad_h, grad)]
        )
    ]
    w_copies = [
        pltpu.make_async_copy(wg, wall.at[:, :, :, :, pl.ds(0, H)], s_w.at[0]),
        pltpu.make_async_copy(wu, wall.at[:, :, :, :, pl.ds(H, H)], s_w.at[1]),
        pltpu.make_async_copy(wd, o_down, s_w.at[2]),
    ]
    for cp in in_copies + w_copies:
        cp.start()
    for cp in in_copies:
        cp.wait()

    r = routing[...]
    g = gates[...]
    r0, r1 = r[0:1, :], r[1:2, :]
    names = iota((E, T), 0)
    c0, c1 = (r0 == names).astype(F32), (r1 == names).astype(F32)
    before = (iota((T, T), 0) < iota((T, T), 1)).astype(BF)
    earlier = mm((c0 + c1).astype(BF), before)
    pos0 = jnp.sum(earlier * c0, axis=0, keepdims=True)
    pos1 = jnp.sum((earlier + c0) * c1, axis=0, keepdims=True)
    key0 = jnp.where(pos0 < CAP, r0.astype(F32) * CAP + pos0, -1.0)
    key1 = jnp.where(pos1 < CAP, r1.astype(F32) * CAP + pos1, -1.0)
    want = iota((MSG, 1), 0).astype(F32)
    m0 = (want == key0).astype(F32)
    m1 = (want == key1).astype(F32)
    gate_slot = jnp.sum(m0 * g[0:1, :] + m1 * g[1:2, :], axis=1, keepdims=True)
    onehot = (m0 + m1).astype(BF)
    gap = jnp.zeros((MSG, G0 - F), F32)
    rows = jnp.concatenate(
        [mm(onehot, acts[...]), gap, mm(onehot, grad[...]) * gate_slot, gap], axis=1
    )
    send[...] = rows.astype(BF).reshape(E, CAP, 128)

    pl.semaphore_wait(barrier, 2 * NY + (NZ - 1) + 2 * (NY - 1) + (NX - 1) + 1)

    unsent = []

    def finish():
        for f in unsent:
            f()

    here = c * NY + y

    def far_copy(k):
        to_y = (y + k) % NY
        return remote(
            send.at[(1 - zh) * NY + to_y], recv.at[here], s_a2a.at[NY + k], r_a2a.at[here],
            dev(x, z4, 1, 1 - zh, to_y),
        )

    def near_copy(k):
        to_y = (y + k) % NY
        return remote(
            send.at[zh * NY + to_y], recv.at[here], s_a2a.at[k], r_a2a.at[here],
            dev(x, z, 0, zh, to_y),
        )

    own_copy = pltpu.make_async_copy(send.at[expert], recv.at[here], s_a2a.at[0])
    for k in range(NY):
        far_copy(k).start()
    for k in (2, 1, 3):
        near_copy(k).start()

    @pl.when(c == 0)
    def _():
        own_copy.start()

    @pl.when(c == 1)
    def _():
        near_copy(0).start()

    def a2a_sent():
        for k in range(NY):
            far_copy(k).wait_send()
        for k in range(1, NY):
            near_copy(k).wait_send()

        @pl.when(c == 1)
        def _():
            near_copy(0).wait_send()

    unsent.append(a2a_sent)

    for cp in w_copies:
        cp.wait()
    for q in range(NX):
        wall[q, :, :, :, pl.ds(2 * H, H)] = o_down[:, pl.ds(q * K, K)].T.reshape(NZ, NC, F, H)
        for cc in range(NC):
            w3[q, cc] = wall[q, :, cc].reshape(ZF, 3 * H).T
    g_r, rest_r = split(iota((MSG, ROWS), 1), 2 * CAP)
    row = iota((MSG, ROWS), 0)
    pick = iota((F, 128), 1) - iota((F, 128), 0)
    put_x = (row == g_r * CAP + rest_r).astype(BF) * (rest_r < CAP).astype(BF)
    put_g = (row == g_r * CAP + rest_r - CAP).astype(BF) * (rest_r >= CAP).astype(BF)
    pick_x, pick_g = (pick == 0).astype(BF), (pick == G0).astype(BF)

    @pl.when(c == 0)
    def _():
        own_copy.wait()

    def a2a_arrived(i, _):
        @pl.when(jnp.logical_or(c == 1, i != here))
        def _():
            remote(recv.at[i], recv.at[i], s_a2a.at[0], r_a2a.at[i], sibling).wait_recv()

        return 0

    lax.fori_loop(0, E, a2a_arrived, 0)
    got = recv[...].reshape(MSG, 128)
    x_t, g_t = nt(pick_x, got).astype(BF), nt(pick_g, got).astype(BF)
    ag[x, z, c] = (mm(x_t, put_x) + mm(g_t, put_g)).astype(BF)

    left, right, far = (x + NX - 1) % NX, (x + 1) % NX, (x + 2) % NX

    def near_z(j):
        return z // HALF * HALF + (z + j * (1 + z % HALF // 2 * 2)) % HALF

    def ag_copy(bx, bz, ss, to):
        blk = ag.at[bx, bz, c]
        return remote(blk, blk, ss, r_ag.at[(bx * NZ + bz) * NC + c], to)

    def ag_arrived(bx, bz, bc):
        blk = ag.at[bx, bz, bc]
        remote(blk, blk, s_agz.at[0], r_ag.at[(bx * NZ + bz) * NC + bc], sibling).wait_recv()

    def hub_copy():
        return ag_copy(x, z, s_agz.at[0], dev(x, z4, c, zh, y))

    def local_copies(bz):
        i = 1 + (bz // HALF + z // HALF) % 2 * (HALF - 1)
        return [
            ag_copy(x, bz, s_agz.at[i + j - 1], dev(x, near_z(j), c, zh, y))
            for j in range(1, HALF)
        ]

    def to_other_core(bx, bz):
        return ag_copy(bx, bz, s_agc.at[bx * NZ + bz], sibling)

    def x_copies_of(bz):
        return [
            ag_copy(x, bz, s_agx.at[bz], dev(right, z, c, zh, y)),
            ag_copy(x, bz, s_agx.at[NZ + bz], dev(left, z, c, zh, y)),
        ]

    def forward_right(bz):
        return ag_copy(left, bz, s_agf.at[bz], dev(right, z, c, zh, y))

    def forward_left(bz):
        return ag_copy(right, bz, s_agf.at[bz], dev(left, z, c, zh, y))

    def unicast(bz):
        return bz // HALF != z // HALF

    def spread(bz):
        @pl.when(unicast(bz))
        def _():
            ag_copy(x, bz, s_agf.at[bz], dev(far, z, c, zh, y)).start()

        for cp in x_copies_of(bz):
            cp.start()
        to_other_core(x, bz).start()

    def z_arrived(bz):
        ag_arrived(x, bz, c)
        spread(bz)

    def x_arrived(bz):
        ag_arrived(left, bz, c)

        @pl.when(jnp.logical_and(bz % 2 == 0, jnp.logical_not(unicast(bz))))
        def _():
            forward_right(bz).start()

        to_other_core(left, bz).start()
        ag_arrived(right, bz, c)

        @pl.when(jnp.logical_and(bz % 2 == 1, jnp.logical_not(unicast(bz))))
        def _():
            forward_left(bz).start()

        to_other_core(right, bz).start()

    def far_arrived(bz):
        ag_arrived(far, bz, c)
        to_other_core(far, bz).start()

    def loop(n, f):
        def step(j, _):
            f(j)
            return 0

        lax.fori_loop(1, n, step, 0)

    def over(j):
        return (near_z(j) + HALF) % NZ

    hub_copy().start()
    for cp in local_copies(z):
        cp.start()
    for cp in x_copies_of(z):
        cp.start()
    to_other_core(x, z).start()
    z_arrived(near_z(1))
    x_arrived(z)
    z_arrived(near_z(2))
    z_arrived(near_z(3))
    ag_arrived(x, z4, c)
    for cp in local_copies(z4):
        cp.start()
    spread(z4)
    loop(HALF, lambda j: x_arrived(near_z(j)))
    loop(HALF, lambda j: z_arrived(over(j)))
    far_arrived(z)
    x_arrived(z4)
    loop(HALF, lambda j: far_arrived(near_z(j)))
    loop(HALF, lambda j: x_arrived(over(j)))
    far_arrived(z4)
    loop(HALF, lambda j: far_arrived(over(j)))

    def gather_sent():
        hub_copy().wait_send()
        for cp in local_copies(z) + local_copies(z4):
            cp.wait_send()

        def x_sent(i, _):
            for cp in x_copies_of(i):
                cp.wait_send()
            forward_right(i).wait_send()
            return 0

        lax.fori_loop(0, NZ, x_sent, 0)

        def c_sent(i, _):
            to_other_core(i // NZ, i % NZ).wait_send()
            return 0

        lax.fori_loop(0, NX * NZ, c_sent, 0)

    unsent.append(gather_sent)
    def block_of(bx, h):
        rows = ag[bx, :, h].reshape(ZF, ROWS)
        return swap_z(rows) if h else rows

    for k in (0, 1, 3, 2):
        bx = (x + k) % NX

        def other_core(i, _):
            ag_arrived(bx, i, 1 - c)
            return 0

        lax.fori_loop(0, NZ, other_core, 0)
        for h in range(NH):
            rows = block_of(bx, h)
            for cc in range(NC):
                new = mm(w3[bx, cc], rows[:, cc * 128 : cc * 128 + W])
                if k:
                    acc[h, cc] += new
                else:
                    acc[h, cc] = new

    both = [acc[h, 0] + pltpu.roll(acc[h, 1], W - G0, 1) for h in range(NH)]
    pre = jnp.concatenate(both, axis=1)
    lane = iota((H, NH * W), 1) & (W - 1)
    is_x = jnp.logical_and(split(lane, 2 * CAP)[1] < CAP, lane < ROWS // 2)
    gate_pre, up_pre = pre[0:H], pre[H : 2 * H]
    grad_hidden = pltpu.roll(pre[2 * H :], NH * W - CAP, 1)
    sig = 1.0 / (1.0 + jnp.exp(-gate_pre))
    act = gate_pre * sig
    zero = jnp.zeros((H, NH * W), F32)
    hidden = jnp.where(is_x, act * up_pre, zero)
    gup = jnp.where(is_x, grad_hidden * act, zero)
    ggp = jnp.where(is_x, grad_hidden * up_pre * sig * (1.0 + gate_pre * (1.0 - sig)), zero)
    gg = jnp.concatenate([ggp, gup], axis=0)
    for h in range(NH):
        own = gg[:, h * W : (h + 1) * W]
        for cc in range(NC):
            shift = h * G0 + cc * CAP
            aw[h, pl.ds(cc * 2 * H, 2 * H), :] = (
                pltpu.roll(own, shift, 1) if shift else own
            ).astype(BF)

    sib_copies = {}
    for k in (2, 1, 3, 0):
        bx = (x + k) % NX
        lhs = jnp.concatenate(
            [wall[bx, :, cc, :, pl.ds(0, 2 * H)].reshape(ZF, 2 * H) for cc in range(NC)], axis=1
        )
        p0, p1 = mm(lhs, aw[0]), swap_z(mm(lhs, aw[1]))
        out = jnp.concatenate([p0[:, 0:128], p0[:, 128:] + p1[:, 0:128], p1[:, 128:]], axis=1)
        part[k] = out.astype(BF).reshape(NQ, NC, F, ROWS)
        cp = remote(part.at[k, :, 1 - c], sib.at[k], s_sib.at[k], r_sib.at[k], sibling)
        cp.start()
        sib_copies[k] = cp

    unsent.append(lambda: [cp.wait_send() for cp in sib_copies.values()])
    def turn(i):
        pair, lower = z // NC, 1 - z // HALF
        if i < NQ // 2:
            return lower * (NQ - 1 - i) + (1 - lower) * i
        return pair if i == NQ - 1 else lower * (1 - pair) + (1 - lower) * (NQ + 1 - pair)

    def cols(p):
        return pl.ds(*PARTS[p])

    def x_copy(k, q, p):
        i = (p * NX + k) * NQ + q
        return remote(
            xs.at[k, q, :, cols(p)], xr.at[k, q, :, cols(p)], s_x.at[i], r_x.at[i],
            dev((x + k) % NX, z, c, zh, y),
        )

    for k in (2, 1, 3, 0):
        sib_copies[k].wait_recv()
        total = part[k, :, c].astype(F32) + sib[k].astype(F32)
        if k:
            xs[k] = total.astype(BF)
            x_copy(k, turn(0), 0).start()
        else:
            zs[...] = total
        if k == 3:
            for p in range(2):
                for i in range(1 - p, NQ):
                    for kk in (2, 1, 3):
                        x_copy(kk, turn(i), p).start()

    def x_left():
        for k in range(1, NX):
            for q in range(NQ):
                for p in range(2):
                    x_copy(k, q, p).wait_send()

    unsent.append(x_left)

    for h in range(NH):
        cut = slice(h * W, (h + 1) * W)
        own = jnp.concatenate([gg[:, cut], pltpu.roll(hidden[:, cut], CAP, 1)], axis=0)
        for cc in range(NC):
            hs[h, cc] = (pltpu.roll(own, G0, 1) if cc else own).T.astype(BF)

    def weight_grads(q):
        downs = []
        rows = [block_of(q, h) for h in range(NH)]
        for cc in range(NC):
            cut = slice(cc * 128, cc * 128 + W)
            out = mm(rows[0][:, cut], hs[0, cc]) + mm(rows[1][:, cut], hs[1, cc])
            out = out.astype(BF).reshape(NZ, F, 3 * H)
            o_gate[q, :, cc] = out[:, :, 0:H]
            o_up[q, :, cc] = out[:, :, H : 2 * H]
            downs.append(out[:, :, 2 * H :])
        o_down[:, pl.ds(q * K, K)] = jnp.stack(downs, axis=1).reshape(K, H).T

    def z_copy(q, p):
        return remote(
            xs.at[0, q, :, cols(p)], zr.at[z, :, cols(p)], s_z.at[p * NQ + q],
            r_z.at[p * NZ + z], dev(x, NC * q + c, c, zh, y),
        )

    for p in range(2):
        for i in range(NQ):
            if p == 0:
                weight_grads(i)
            q = turn(i)
            for k in (2, 1, 3):
                x_copy(k, q, p).wait_recv()
            total = zs[q, :, cols(p)]
            for k in (1, 2, 3):
                total += xr[k, q, :, cols(p)].astype(F32)
            xs[0, q, :, cols(p)] = total.astype(BF)

            @pl.when(NC * q + c != z)
            def _():
                z_copy(q, p).start()

    def z_sent():
        for q in range(NQ):
            @pl.when(NC * q + c != z)
            def _():
                for p in range(2):
                    z_copy(q, p).wait_send()

    unsent.append(z_sent)
    def back_copy(h, k, cc):
        to_y = (y + k) % NY
        i = (h * NY + k) * NC + cc
        to = dev(x, z4, cc, 1 - zh, to_y) if h else dev(x, z, cc, zh, to_y)
        return remote(
            back_s.at[(h * NY + to_y) * NC + cc], back_r.at[expert],
            s_back.at[i], r_back.at[expert], to,
        )

    own_back = remote(
        back_s.at[y * NC + 1 - c], back_r.at[expert], s_back.at[0], r_back.at[expert], sibling
    )
    back_list = [(h, k, cc) for h in (1, 0) for k in range(NY) for cc in range(NC) if h or k]

    @pl.when(z % NC == c)
    def _():
        eye_f = (iota((W, W), 0) == iota((W, W), 1)).astype(BF)
        for p in range(2):
            zr[z, :, cols(p)] = xs[0, z // NC, :, cols(p)]
            for k in range(1, NZ):
                bz = (z + k) % NZ
                blk = zr.at[bz, :, cols(p)]
                remote(blk, blk, s_z.at[0], r_z.at[p * NZ + bz], sibling).wait_recv()
            h = 1 - p
            total = jnp.sum(zr[:, :, h * 128 : h * 128 + W].astype(F32), axis=0).astype(BF)
            wide = jnp.concatenate([total, jnp.zeros((128 - F, W), BF)], axis=0)
            rows = nt(eye_f, wide)[h * G0 : h * G0 + MSG]
            back_s[h * E : (h + 1) * E] = rows.astype(BF).reshape(E, CAP, 128)
            for args in back_list:
                if args[0] == h:
                    back_copy(*args).start()
        own_back.start()
        back_r[expert] = back_s[y * NC + c]

    def back_sent():
        @pl.when(z % NC == c)
        def _():
            for args in back_list:
                back_copy(*args).wait_send()
            own_back.wait_send()

    unsent.append(back_sent)

    eye = (iota((T, T), 0) == iota((T, T), 1)).astype(F32)

    def as_col(row):
        return jnp.sum(eye * row, axis=1, keepdims=True)

    want_r = iota((1, MSG), 1).astype(F32)
    combine = jnp.logical_or(want_r == as_col(key0), want_r == as_col(key1)).astype(BF)

    def back_arrived(i, _):
        @pl.when(jnp.logical_or(z % NC != c, i != expert))
        def _():
            remote(back_r.at[i], back_r.at[i], s_back.at[0], r_back.at[i], sibling).wait_recv()

        return 0

    lax.fori_loop(0, E, back_arrived, 0)
    o_acts[...] = mm(combine, back_r[...].reshape(MSG, 128))[:, 0:F].astype(BF)

    finish()


def put(*refs):
    n = len(refs) // 2
    sems = refs[-1]
    copies = [pltpu.make_async_copy(refs[i], refs[n + i], sems.at[i]) for i in range(n)]
    for cp in copies:
        cp.start()
    for cp in copies:
        cp.wait()


def body(acts, grad_out, routing, gates, w_gate, w_up, w_down):
    d = NX * K
    vm = pl.BlockSpec(memory_space=pltpu.VMEM)
    hbm = pl.BlockSpec(memory_space=pltpu.HBM)
    dma = pltpu.SemaphoreType.DMA
    shapes = (
        jax.ShapeDtypeStruct((NX, NZ, NC, F, H), BF),
        jax.ShapeDtypeStruct((NX, NZ, NC, F, H), BF),
        jax.ShapeDtypeStruct((H, d), BF),
        jax.ShapeDtypeStruct((T, F), BF),
    )
    out = pl.pallas_call(
        kernel,
        name="experts_backward",
        out_shape=shapes,
        in_specs=[hbm] * 7,
        out_specs=(vm,) * 4,
        scratch_shapes=[
            pltpu.VMEM((T, F), BF),
            pltpu.VMEM((T, F), BF),
            pltpu.VMEM((2, T), jnp.int32),
            pltpu.VMEM((2, T), F32),
            pltpu.VMEM((NX, NZ, NC, F, 3 * H), BF),
            pltpu.VMEM((NX, NC, 3 * H, ZF), BF),
            pltpu.VMEM((E, CAP, 128), BF),
            pltpu.VMEM((E, CAP, 128), BF),
            pltpu.VMEM((NX, NZ, NC, F, ROWS), BF),
            pltpu.VMEM((NH, NC, 3 * H, W), F32),
            pltpu.VMEM((NH, NC * 2 * H, W), BF),
            pltpu.VMEM((NH, NC, W, 3 * H), BF),
            pltpu.VMEM((NX, NQ, NC, F, ROWS), BF),
            pltpu.VMEM((NX, NQ, F, ROWS), BF),
            pltpu.VMEM((NX, NQ, F, ROWS), BF),
            pltpu.VMEM((NX, NQ, F, ROWS), BF),
            pltpu.VMEM((NQ, F, ROWS), F32),
            pltpu.VMEM((NZ, F, ROWS), BF),
            pltpu.VMEM((E * NC, CAP, 128), BF),
            pltpu.VMEM((E, CAP, 128), BF),
            dma((4,)),
            dma((3,)),
            dma((E,)),
            dma((E,)),
            dma((NX * NZ * NC,)),
            dma((2 * HALF - 1,)),
            dma((2 * NZ,)),
            dma((NZ,)),
            dma((NX * NZ,)),
            dma((NX,)),
            dma((NX,)),
            dma((2 * NX * NQ,)),
            dma((2 * NX * NQ,)),
            dma((2 * NQ,)),
            dma((2 * NZ,)),
            dma((E * NC,)),
            dma((E,)),
        ],
        compiler_params=pltpu.CompilerParams(
            collective_id=0, has_side_effects=True, vmem_limit_bytes=40 << 20
        ),
    )(
        *[
            pltpu.with_memory_space_constraint(a, pltpu.HBM)
            for a in (
                acts,
                grad_out,
                routing.T,
                gates.T,
                w_gate.reshape(NX, NZ, NC, F, H),
                w_up.reshape(NX, NZ, NC, F, H),
                w_down.reshape(H, d),
            )
        ]
    )
    shapes = (jax.ShapeDtypeStruct((d, H), BF),) * 2 + shapes[2:]
    out = pl.pallas_call(
        put,
        name="put",
        out_shape=shapes,
        in_specs=[pl.BlockSpec(memory_space=pl.ANY)] * 4,
        out_specs=(hbm,) * 4,
        scratch_shapes=[dma((4,))],
        compiler_params=pltpu.CompilerParams(vmem_limit_bytes=1 << 20),
    )(out[0].reshape(d, H), out[1].reshape(d, H), out[2], out[3])
    return (out[0][None], out[1][None], out[2][None], out[3])


def solution(mesh):
    return jax.shard_map(
        body,
        mesh=mesh,
        in_specs=(
            P("expert", "tensor"),
            P("expert", "tensor"),
            P("expert", None),
            P("expert", None),
            P("expert", None, "tensor"),
            P("expert", None, "tensor"),
            P("expert", "tensor", None),
        ),
        out_specs=(
            P("expert", None, "tensor"),
            P("expert", None, "tensor"),
            P("expert", "tensor", None),
            P("expert", "tensor"),
        ),
        check_vma=False,
    )
```
